512 devices in a mesh: terms: 32 (over y_hi, z), rows: 4 (over y_lo, core), cols: 4 (over x).
Axes of the slice: x: 4, y: 8 (y_hi: 4, y_lo: 2; y = y_hi * 2 + y_lo), z: 8, core: 2. Of those that a mesh axis runs over, the one named last changes fastest.
Arguments:
- wavefunction: bfloat16 [2, 1024, 1024], P(None, 'rows', 'cols'), may hold values from -6 to 6
- energy: float32 [2], replicated, may hold values from 1 to 4
- block_rows: int32 [2], replicated, may hold values from 512 to 1024
- block_cols: int32 [2], replicated, may hold values from 512 to 1024
- left_ops: bfloat16 [128, 1024, 1024], P('terms', 'rows'), may hold values from -0.1875 to 0.1875
- right_ops: bfloat16 [128, 1024, 1024], P('terms', 'cols'), may hold values from -0.1875 to 0.1875
- source: int32 [128], P('terms'), may hold values from 0 to 1
- target: int32 [128], P('terms'), may hold values from 0 to 1
Outputs:
- sigma: bfloat16 [2, 1024, 1024], P(None, 'rows', 'cols')
- residual: bfloat16 [2, 1024, 1024], P(None, 'rows', 'cols')
The draws below stay inside these ranges and needn't reach their ends.
Inputs may be any that keep to these rules, and one draw needn't show every extreme that they name: source[t] is the sector whose block term t reads. target[t] is the sector to which term t adds. `block_rows`: entries of a sector block beyond its live left or right states are ignored.
All inputs are finite; a program needn't handle non-finite values.
Results may differ from the reference program's by a relative error of at most 0.0044.
The reference program's roundings to bfloat16 on the way count: a program that leaves them out, or rounds other values in their place, can miss the bound.
Values may be sent and summed in bfloat16 or wider, within the bound.
A program may use at most 64 MiB of HBM per device.

```python
import math
import jax
import jax.numpy as jnp
import numpy as np
from jax import lax

BLK = 1024
NSEC = 2
TERMS = 128


def plant(array, own_key, smallest, top_value):
    shape = array.shape
    index_at = [jax.random.randint(jax.random.fold_in(own_key, axis), (), 0, shape[axis]) for axis in range(len(shape))]
    array = array.at[tuple(index_at)].set(smallest)
    longest = shape.index(max(shape))
    index_at[longest] = (index_at[longest] + 1) % shape[longest]
    return array.at[tuple(index_at)].set(top_value)


def block_scale(key, dims, pieces, least, largest):
    factor_of, own = 1.0, jax.random.fold_in(key, 6)
    for axis_at, parts in pieces:
        steps = jnp.exp(jax.random.uniform(jax.random.fold_in(own, axis_at), (parts,), jnp.float32, least / len(pieces), largest / len(pieces)))
        factor_of = factor_of * jnp.repeat(steps, dims[axis_at] // parts).reshape([-1 if axis == axis_at else 1 for axis in range(len(dims))])
    return factor_of


def cumulative_ranks(count, slope):
    weights = [(1 << 20) // math.isqrt(standing ** slope) + 1 for standing in range(1, count + 1)]
    scale = 1 + sum(weights) // (1 << 30)
    return np.cumsum(np.array([max(1, weight // scale) for weight in weights]))


def skewed_ids(rng, dims, amount, slope):
    listing = cumulative_ranks(amount, slope)
    ticket = jax.random.randint(jax.random.fold_in(rng, 1), dims, 0, int(listing[amount - 1]))
    rank = jnp.searchsorted(jnp.asarray(listing, jnp.int32), ticket, side="right")
    return jax.random.permutation(jax.random.fold_in(rng, 2), amount)[rank].astype(jnp.int32)


def bell_draw(stream_key, extent, scale, bound, cuts=(), kind=jnp.bfloat16):
    array = jax.random.normal(stream_key, extent, jnp.float32) * scale
    if len(cuts) > 0:
        array = block_scale(stream_key, extent, cuts, -0.22, 0.18) * array
    return jnp.clip(array, min=-bound, max=bound).astype(kind)


def setup_inputs(seed: int = 0) -> dict:
    seeds = jax.random.split(jax.random.key(seed), 9)
    return {
        "wavefunction": bell_draw(seeds[0], (NSEC, BLK, BLK), 1.0, 6.0, ((1, 4), (2, 4))),
        "energy": jnp.clip(jnp.exp(jax.random.uniform(seeds[1], (NSEC,), jnp.float32, math.log(1.0), math.log(4.0))), 1.0, 4.0),
        "block_rows": jax.random.randint(seeds[2], (NSEC,), BLK // 2, BLK + 1).astype(jnp.int32),
        "block_cols": jax.random.randint(seeds[3], (NSEC,), BLK // 2, BLK + 1).astype(jnp.int32),
        "left_ops": bell_draw(seeds[4], (TERMS, BLK, BLK), BLK ** -0.5, 0.1875, ((0, 32), (1, 4))),
        "right_ops": bell_draw(seeds[5], (TERMS, BLK, BLK), BLK ** -0.5, 0.1875, ((0, 32), (1, 4))),
        "source": plant(jax.random.randint(seeds[6], (TERMS,), 0, NSEC), jax.random.fold_in(seeds[6], 1), 0, NSEC - 1).astype(jnp.int32),
        "target": plant(skewed_ids(seeds[7], (TERMS,), NSEC, 2), jax.random.fold_in(seeds[7], 3), 0, NSEC - 1).astype(jnp.int32),
    }


def reference(wavefunction, energy, block_rows, block_cols, left_ops, right_ops, source, target):
    positions = jnp.arange(BLK, dtype=jnp.int32)
    inside = (positions[None, :, None] < block_rows[:, None, None]) & (positions[None, None, :] < block_cols[:, None, None])
    live_psi = jnp.where(inside, wavefunction, jnp.zeros_like(wavefunction))
    sector_ids = jnp.arange(NSEC, dtype=jnp.int32)

    def add_term(running, scanned):
        left_op, right_op, src_sector, dst_sector = scanned
        src_block = lax.dynamic_index_in_dim(live_psi, src_sector, 0, keepdims=False)
        products = jnp.dot(left_op, src_block, preferred_element_type=jnp.float32).astype(jnp.bfloat16)
        addition = lax.dot_general(products, right_op, (((1,), (1,)), ((), ())), preferred_element_type=jnp.float32)
        hit = (sector_ids == dst_sector)[:, None, None]
        return running + jnp.where(hit, addition[None], jnp.zeros_like(addition[None])), None

    start_sum = jnp.zeros((NSEC, BLK, BLK), jnp.float32)
    summed, unused = lax.scan(add_term, start_sum, (left_ops, right_ops, source, target))
    live_f = live_psi.astype(jnp.float32)
    full_sigma = jnp.where(inside, summed + energy[:, None, None] * live_f, jnp.zeros_like(summed))
    numerator = jnp.sum(live_f * full_sigma)
    denominator = jnp.sum(live_f * live_f)
    rayleigh = numerator / (denominator + 1e-6)
    residual = full_sigma - rayleigh * live_f
    return full_sigma.astype(jnp.bfloat16), residual.astype(jnp.bfloat16)
```

```python
import functools

import jax
import jax.numpy as jnp
from jax import lax
from jax.experimental import pallas as pl
from jax.experimental.pallas import tpu as pltpu
from jax.sharding import PartitionSpec as P

MESH = pl.DeviceIdType.MESH
EPSILON = 1e-06
F32 = jnp.float32
BF16 = jnp.bfloat16
N_SEMS = 96


class Copies:
    def __init__(self, send_sems, recv_sems):
        self.send_sems, self.recv_sems, self.used, self.open = send_sems, recv_sems, 0, []

    def send(self, src, dst, device):
        at = self.used
        self.used += 1
        copy = pltpu.make_async_remote_copy(
            src, dst, self.send_sems.at[at], self.recv_sems.at[at], device_id=device, device_id_type=MESH
        )
        copy.start()
        self.open.append(copy)
        return copy

    def finish(self):
        for copy in self.open:
            copy.wait_send()


def kernel(
    source, target, block_rows, block_cols, energy, psi, left, right,
    sigma, residual,
    psi0, psi1, psi2, psi3, lbuf, rbuf, adds, part, part_b, zbuf, ybuf, summed, own,
    tile1, tile2, tile3, tile4, local_sems, send_sems, recv_sems,
):
    t, r, x = lax.axis_index("terms"), lax.axis_index("rows"), lax.axis_index("cols")
    yhi, z, ylo, core = t // 8, t % 8, r // 2, r % 2
    parity = z % 2

    def at_y(dy):
        y = (yhi * 2 + ylo + dy + 8) % 8
        return {"terms": (y // 2) * 8 + z, "rows": (y % 2) * 2 + core}

    def at_z(dz):
        return {"terms": yhi * 8 + (z + dz + 8) % 8}

    def at_yhi(d):
        return {"terms": ((yhi + d + 4) % 4) * 8 + z}

    def at_x(dx):
        return {"cols": (x + dx + 4) % 4}

    def at_r(d):
        return {"rows": (r + d) % 4}

    partner = {"rows": ylo * 2 + 1 - core}
    z_steps = (4, 3, -3, 2, -2, 1, -1)
    y_steps = (2, 1, -1)
    x_steps = (1, -1, 2)

    barrier = pltpu.get_barrier_semaphore()
    friends = [partner, at_y(1), at_y(-1)]
    friends += [{"rows": (1 - ylo) * 2 + 1 - core}]
    friends += [at_x(d) for d in x_steps] + [at_z(d) for d in z_steps] + [at_yhi(d) for d in y_steps]
    for friend in friends:
        pl.semaphore_signal(barrier, inc=1, device_id=friend, device_id_type=MESH)

    psis = {0: psi0, 1: psi1, 2: psi2, 3: psi3}
    mine = pl.multiple_of(r * 256, 256)
    theirs = pl.multiple_of(((1 - ylo) * 2 + core) * 256, 256)
    native = pltpu.make_async_copy(psi, psi0.at[:, pl.ds(mine, 256), :], local_sems.at[0])
    native.start()
    load_l = pltpu.make_async_copy(left, lbuf, local_sems.at[1])
    load_l.start()
    load_r = pltpu.make_async_copy(right, rbuf, local_sems.at[2])
    load_r.start()
    pl.semaphore_wait(barrier, len(friends))

    copies = Copies(send_sems, recv_sems)
    send = copies.send

    def unit(k, sector, base, half=None):
        if half is None:
            return psis[k].at[sector, pl.ds(base, 256), :]
        return psis[k].at[sector, pl.ds(pl.multiple_of(base + 128 * half, 128), 128), :]

    a_in = {}
    a_in[3] = send(psi.at[parity], unit(3, parity, mine), at_x(1))
    a_in[1] = send(psi.at[parity], unit(1, parity, mine), at_x(-1))
    y_in = [send(psi.at[0], unit(0, 0, mine), at_y(1)), send(psi.at[1], unit(0, 1, mine), at_y(-1))]
    a_in[2] = send(psi.at[parity], unit(2, parity, mine), at_x(2))
    arrivals = {0: [], 1: [], 2: [], 3: []}
    arrivals[0].append(send(psi, psi0.at[:, pl.ds(mine, 256), :], partner))

    def share(k, ref):
        arrivals[k].append(send(ref, ref, partner))

    b_in, c_in = {}, {}

    def pass_on(k):
        a_in[k].wait_recv()
        b_in[k], c_in[k] = [], []
        for half, way in ((0, 1), (1, -1)):
            piece = unit(k, parity, mine, half)
            c_in[k].append(send(piece, piece, at_y(way)))
            b_in[k].append(send(piece, piece, at_z(way)))
        share(k, unit(k, parity, mine))

    d_in = {}

    def turn(k):
        d_in[k] = []
        for half, way in ((0, 1), (1, -1)):
            c_in[k][half].wait_recv()
            piece = unit(k, parity, theirs, half)
            d_in[k].append(send(piece, piece, at_z(way)))
            share(k, piece)

    def take_b(k):
        for half in (0, 1):
            b_in[k][half].wait_recv()
            share(k, unit(k, 1 - parity, mine, half))

    def take_d(k):
        for half in (0, 1):
            d_in[k][half].wait_recv()
            share(k, unit(k, 1 - parity, theirs, half))

    def settle(k):
        for copy in arrivals[k]:
            copy.wait_recv()

    def mask_left():
        load_l.wait()
        columns = lax.broadcasted_iota(jnp.int32, (256, 1024), 1)

        def one(i, carry):
            lbuf[i] = jnp.where(columns < block_rows[source[i]], lbuf[i], jnp.zeros((), BF16))
            return carry

        lax.fori_loop(0, 4, one, 0)

    def compute(k, first):
        start = pl.multiple_of(((x + k) % 4) * 256, 256)
        columns = lax.broadcasted_iota(jnp.int32, (256, 256), 1) + start

        def one(i, carry):
            sector = source[i]
            product = jnp.dot(lbuf[i], psis[k][sector], preferred_element_type=F32)
            product = jnp.where(columns < block_cols[sector], product, 0.0).astype(BF16)
            added = lax.dot_general(
                product, rbuf[i, :, pl.ds(start, 256)], (((1,), (1,)), ((), ())), preferred_element_type=F32
            )
            adds[i] = added if first else adds[i] + added
            return carry

        lax.fori_loop(0, 4, one, 0)

    mask_left()
    pass_on(1)
    pass_on(3)
    for s in (0, 1):
        y_in[s].wait_recv()
        share(0, unit(0, s, theirs))
    turn(1)
    take_b(1)
    pass_on(2)
    turn(3)
    take_b(3)
    native.wait()
    settle(0)
    load_r.wait()
    compute(0, True)
    turn(2)
    take_d(1)
    take_b(2)
    settle(1)
    compute(1, False)
    take_d(3)
    settle(3)
    compute(3, False)
    take_d(2)
    settle(2)
    compute(2, False)

    rows = lax.broadcasted_iota(jnp.int32, (256, 256), 0) + r * 256
    columns = lax.broadcasted_iota(jnp.int32, (256, 256), 1) + x * 256
    numerator = jnp.zeros((8, 256), F32)
    denominator = jnp.zeros((8, 256), F32)
    for s in (0, 1):
        block = jnp.where(target[0] == s, adds[0], 0.0)
        for i in (1, 2, 3):
            block = block + jnp.where(target[i] == s, adds[i], 0.0)
        part[pl.ds(s * 256, 256), :] = block
        part_b[pl.ds(s * 256, 256), :] = block.astype(BF16)
    z_in = []
    for d in z_steps:
        there = pl.multiple_of(((z + d + 8) % 8) * 64, 64)
        z_in.append(send(part_b.at[pl.ds(there, 64), :], zbuf.at[z], at_z(d)))
    for s in (0, 1):
        inside = (rows < block_rows[s]) & (columns < block_cols[s])
        live = jnp.where(inside, psi0[s, pl.ds(mine, 256), :].astype(F32), 0.0)
        own[s] = live
        square = jnp.sum((live * live).reshape(32, 8, 256), axis=0) * (1.0 / 32)
        block = part[pl.ds(s * 256, 256), :]
        numerator += jnp.sum((live * block).reshape(32, 8, 256), axis=0) + energy[s] * square
        denominator += square

    def exchange(value, tiles, here, moves):
        tiles[here] = value
        got = [send(tiles.at[here], tiles.at[here], device) for device in moves]

        def total():
            for copy in got:
                copy.wait_recv()
            whole = tiles[0]
            for i in range(1, tiles.shape[0]):
                whole = whole + tiles[i]
            return whole

        return total

    sums = jnp.concatenate([numerator, denominator], axis=0)
    sums = sums[:, :128] + sums[:, 128:]
    sums = exchange(sums, tile1, r, [at_r(d) for d in (1, 2, 3)])()
    sums_later = exchange(sums, tile2, z, [at_z(d) for d in z_steps])

    for copy in z_in:
        copy.wait_recv()
    here = pl.multiple_of(z * 64, 64)
    total = part[pl.ds(here, 64), :]
    for d in z_steps:
        total = total + zbuf[(z + d + 8) % 8].astype(F32)
    ybuf[yhi] = total.astype(BF16)
    y_got = [send(ybuf.at[yhi], ybuf.at[yhi], at_yhi(d)) for d in y_steps]
    sums_later = exchange(sums_later(), tile3, yhi, [at_yhi(d) for d in y_steps])
    for copy in y_got:
        copy.wait_recv()
    total = ybuf[0].astype(F32)
    for i in (1, 2, 3):
        total = total + ybuf[i].astype(F32)
    summed[pl.ds(here, 64), :] = total.astype(BF16)
    chunk = summed.at[pl.ds(here, 64), :]
    last = [send(chunk, chunk, at_z(d)) for d in z_steps]
    sums = exchange(sums_later(), tile4, x, [at_x(d) for d in x_steps])()
    rayleigh = jnp.sum(sums[:8]) / (jnp.sum(sums[8:]) + EPSILON)
    for copy in last:
        copy.wait_recv()
    for s in (0, 1):
        inside = (rows < block_rows[s]) & (columns < block_cols[s])
        live = own[s]
        full = jnp.where(inside, summed[pl.ds(s * 256, 256), :].astype(F32) + energy[s] * live, 0.0)
        sigma[s] = full.astype(BF16)
        residual[s] = (full - rayleigh * live).astype(BF16)
    copies.finish()


def per_device(wavefunction, energy, block_rows, block_cols, left_ops, right_ops, source, target):
    smem = pl.BlockSpec(memory_space=pltpu.SMEM)
    anyw = pl.BlockSpec(memory_space=pl.ANY)
    vmem = pl.BlockSpec(memory_space=pltpu.VMEM)
    block = jax.ShapeDtypeStruct((2, 256, 256), BF16)
    return pl.pallas_call(
        kernel,
        out_shape=(block, block),
        in_specs=[smem] * 5 + [anyw] * 3,
        out_specs=(vmem, vmem),
        scratch_shapes=[pltpu.VMEM((2, 1024, 256), BF16)] * 4
        + [
            pltpu.VMEM((4, 256, 1024), BF16),
            pltpu.VMEM((4, 256, 1024), BF16),
            pltpu.VMEM((4, 256, 256), F32),
            pltpu.VMEM((512, 256), F32),
            pltpu.VMEM((512, 256), BF16),
            pltpu.VMEM((8, 64, 256), BF16),
            pltpu.VMEM((4, 64, 256), BF16),
            pltpu.VMEM((512, 256), BF16),
            pltpu.VMEM((2, 256, 256), F32),
            pltpu.VMEM((4, 16, 128), F32),
            pltpu.VMEM((8, 16, 128), F32),
            pltpu.VMEM((4, 16, 128), F32),
            pltpu.VMEM((4, 16, 128), F32),
            pltpu.SemaphoreType.DMA((3,)),
            pltpu.SemaphoreType.DMA((N_SEMS,)),
            pltpu.SemaphoreType.DMA((N_SEMS,)),
        ],
        compiler_params=pltpu.CompilerParams(
            collective_id=0, has_side_effects=True, vmem_limit_bytes=40 * 1024 * 1024
        ),
        name="sigma_step",
    )(source, target, block_rows, block_cols, energy, wavefunction, left_ops, right_ops)


def solution(mesh):
    in_specs = (
        P(None, "rows", "cols"),
        P(),
        P(),
        P(),
        P("terms", "rows", None),
        P("terms", "cols", None),
        P("terms"),
        P("terms"),
    )
    out_specs = (P(None, "rows", "cols"), P(None, "rows", "cols"))
    return jax.shard_map(per_device, mesh=mesh, in_specs=in_specs, out_specs=out_specs, check_vma=False)
```

```python
import functools

import jax
import jax.numpy as jnp
from jax import lax
from jax.experimental import pallas as pl
from jax.experimental.pallas import tpu as pltpu
from jax.sharding import PartitionSpec as P

MESH = pl.DeviceIdType.MESH
EPSILON = 1e-06
F32 = jnp.float32
BF16 = jnp.bfloat16
N_SEMS = 120
VMEM_LIMIT = 67043328


class Copies:
    def __init__(self, send_sems, recv_sems):
        self.send_sems, self.recv_sems, self.used, self.open = send_sems, recv_sems, 0, []

    def send(self, src, dst, device):
        at = self.used
        self.used += 1
        copy = pltpu.make_async_remote_copy(
            src, dst, self.send_sems.at[at], self.recv_sems.at[at], device_id=device, device_id_type=MESH
        )
        copy.start()
        self.open.append(copy)
        return copy

    def finish(self):
        for copy in self.open:
            copy.wait_send()


def kernel(
    source_in, target_in, rows_in, cols_in, energy_in, psi, left, right,
    sigma, residual,
    source, target, block_rows, block_cols, energy,
    psi0, psi1, psi2, psi3, lbuf, rbuf, adds, part, part_b, zbuf, ybuf, summed, own,
    tile1, tile2, tile3, tile4, local_sems, send_sems, recv_sems, hello,
):
    t, r, x = lax.axis_index("terms"), lax.axis_index("rows"), lax.axis_index("cols")
    yhi, z, ylo, core = t // 8, t % 8, r // 2, r % 2
    parity = z % 2

    def at_y(dy):
        y = (yhi * 2 + ylo + dy + 8) % 8
        return {"terms": (y // 2) * 8 + z, "rows": (y % 2) * 2 + core}

    def at_z(dz):
        return {"terms": yhi * 8 + (z + dz + 8) % 8}

    def at_yhi(d):
        return {"terms": ((yhi + d + 4) % 4) * 8 + z}

    def at_x(dx):
        return {"cols": (x + dx + 4) % 4}

    def at_r(d):
        return {"rows": (r + d) % 4}

    partner = {"rows": ylo * 2 + 1 - core}
    z_steps = (4, 3, -3, 2, -2, 1, -1)
    y_steps = (2, 1, -1)
    x_steps = (1, -1, 2)

    def greet(sem, friends):
        for friend in friends:
            pl.semaphore_signal(sem, inc=1, device_id=friend, device_id_type=MESH)

    line = [at_y(1), at_y(-1), at_z(1), at_z(-1)]
    near = [partner, at_x(1), at_x(-1)] + line
    barrier = pltpu.get_barrier_semaphore()
    greet(barrier, near)

    psis = {0: psi0, 1: psi1, 2: psi2, 3: psi3}
    mine = pl.multiple_of(r * 256, 256)
    theirs = pl.multiple_of(((1 - ylo) * 2 + core) * 256, 256)
    tables = ((source_in, source), (target_in, target), (rows_in, block_rows), (cols_in, block_cols), (energy_in, energy))
    small = [pltpu.make_async_copy(a, b, local_sems.at[3 + i]) for i, (a, b) in enumerate(tables)]
    for copy in small:
        copy.start()
    native = pltpu.make_async_copy(psi, psi0.at[:, pl.ds(mine, 256), :], local_sems.at[0])
    native.start()
    load_l = pltpu.make_async_copy(left, lbuf, local_sems.at[1])
    load_l.start()
    load_r = pltpu.make_async_copy(right, rbuf, local_sems.at[2])
    load_r.start()
    pl.semaphore_wait(barrier, len(near))
    greet(hello.at[0], near)

    copies = Copies(send_sems, recv_sems)
    send = copies.send

    def unit(k, sector, base, half=None):
        if half is None:
            return psis[k].at[sector, pl.ds(base, 256), :]
        return psis[k].at[sector, pl.ds(pl.multiple_of(base + 128 * half, 128), 128), :]

    arrivals = {0: [], 1: [], 2: [], 3: []}
    a_in = {1: [], 2: [], 3: []}
    b_in = {1: [], 2: [], 3: []}
    c_in = {1: [], 2: [], 3: []}
    d_in = {1: [], 2: [], 3: []}
    y_in = {0: [], 1: []}
    for half in (0, 1):
        rows = pl.ds(128 * half, 128)
        a_in[3].append(send(psi.at[parity, rows, :], unit(3, parity, mine, half), at_x(1)))
        a_in[1].append(send(psi.at[parity, rows, :], unit(1, parity, mine, half), at_x(-1)))
        y_in[0].append(send(psi.at[0, rows, :], unit(0, 0, mine, half), at_y(1)))
        y_in[1].append(send(psi.at[1, rows, :], unit(0, 1, mine, half), at_y(-1)))
    arrivals[0].append(send(psi, psi0.at[:, pl.ds(mine, 256), :], partner))

    def share(k, ref):
        arrivals[k].append(send(ref, ref, partner))

    def settle(k):
        for copy in arrivals[k]:
            copy.wait_recv()

    def compute(k, first):
        start = pl.multiple_of(((x + k) % 4) * 256, 256)
        columns = lax.broadcasted_iota(jnp.int32, (256, 256), 1) + start

        def one(i, carry):
            sector = source[i]
            product = jnp.dot(lbuf[i], psis[k][sector], preferred_element_type=F32)
            product = jnp.where(columns < block_cols[sector], product, 0.0).astype(BF16)
            added = lax.dot_general(
                product, rbuf[i, :, pl.ds(start, 256)], (((1,), (1,)), ((), ())), preferred_element_type=F32
            )
            adds[i] = added if first else adds[i] + added
            return carry

        lax.fori_loop(0, 4, one, 0)

    for copy in small:
        copy.wait()
    load_l.wait()
    depth = lax.broadcasted_iota(jnp.int32, (256, 1024), 1)

    def mask_one(i, carry):
        lbuf[i] = jnp.where(depth < block_rows[source[i]], lbuf[i], jnp.zeros((), BF16))
        return carry

    lax.fori_loop(0, 4, mask_one, 0)

    ways = (1, -1)
    for half, k in ((0, 3), (0, 1), (1, 1), (1, 3)):
        a_in[k][half].wait_recv()
        piece = unit(k, parity, mine, half)
        if (half, k) in ((0, 3), (1, 1)):
            a_in[2].append(send(piece, unit(2, parity, mine, half), at_x(ways[half])))
        b_in[k].append(send(piece, piece, at_z(ways[half])))
    for k in (1, 3):
        share(k, unit(k, parity, mine))
    pl.semaphore_wait(hello.at[0], len(near))
    greet(hello.at[1], line)
    for half in (0, 1):
        for s in (0, 1):
            y_in[s][half].wait_recv()
        piece = unit(0, parity, theirs, half)
        c_in[3].append(send(piece, unit(3, parity, theirs, half), at_x(1)))
        c_in[1].append(send(piece, unit(1, parity, theirs, half), at_x(-1)))
    for s in (0, 1):
        share(0, unit(0, s, theirs))
    for half in (0, 1):
        a_in[2][half].wait_recv()
        piece = unit(2, parity, mine, half)
        c_in[2].append(send(piece, piece, at_y(ways[half])))
        b_in[2].append(send(piece, piece, at_z(ways[half])))
    share(2, unit(2, parity, mine))
    for half, k in ((0, 3), (0, 1), (1, 1), (1, 3)):
        b_in[k][half].wait_recv()
        piece = unit(k, 1 - parity, mine, half)
        d_in[k].append(send(piece, piece, at_y(ways[half])))
    for k in (1, 3):
        share(k, unit(k, 1 - parity, mine))
    pl.semaphore_wait(hello.at[1], len(line))
    greet(hello.at[2], line)
    for half in (0, 1):
        c_in[2][half].wait_recv()
        piece = unit(2, parity, theirs, half)
        d_in[2].append(send(piece, piece, at_z(ways[half])))
    share(2, unit(2, parity, theirs))
    for k in (1, 3):
        for half in (0, 1):
            c_in[k][half].wait_recv()
        share(k, unit(k, parity, theirs))
    for half in (0, 1):
        b_in[2][half].wait_recv()
    share(2, unit(2, 1 - parity, mine))
    native.wait()
    settle(0)
    load_r.wait()
    compute(0, True)
    for k in (1, 3):
        for half in (0, 1):
            d_in[k][half].wait_recv()
        share(k, unit(k, 1 - parity, theirs))
    pl.semaphore_wait(hello.at[2], len(line))
    for half in (0, 1):
        d_in[2][half].wait_recv()
    share(2, unit(2, 1 - parity, theirs))
    settle(1)
    compute(1, False)
    settle(3)
    compute(3, False)
    settle(2)
    compute(2, False)

    rows = lax.broadcasted_iota(jnp.int32, (256, 256), 0) + r * 256
    columns = lax.broadcasted_iota(jnp.int32, (256, 256), 1) + x * 256
    z_in = {0: [], 1: []}
    for s in (0, 1):
        block = jnp.where(target[0] == s, adds[0], 0.0)
        for i in (1, 2, 3):
            block = block + jnp.where(target[i] == s, adds[i], 0.0)
        part[s] = block
        part_b[s] = block.astype(BF16)
        for d in z_steps:
            there = pl.multiple_of(((z + d + 8) % 8) * 32, 32)
            z_in[s].append(send(part_b.at[s, pl.ds(there, 32), :], zbuf.at[s, z], at_z(d)))
    numerator = jnp.zeros((8, 256), F32)
    denominator = jnp.zeros((8, 256), F32)
    for s in (0, 1):
        inside = (rows < block_rows[s]) & (columns < block_cols[s])
        live = jnp.where(inside, psi0[s, pl.ds(mine, 256), :].astype(F32), 0.0)
        own[s] = live
        square = jnp.sum((live * live).reshape(32, 8, 256), axis=0) * (1.0 / 32)
        numerator += jnp.sum((live * part[s]).reshape(32, 8, 256), axis=0) + energy[s] * square
        denominator += square

    def exchange(value, tiles, here, moves):
        tiles[here] = value
        got = [send(tiles.at[here], tiles.at[here], device) for device in moves]

        def total():
            for copy in got:
                copy.wait_recv()
            whole = tiles[0]
            for i in range(1, tiles.shape[0]):
                whole = whole + tiles[i]
            return whole

        return total

    sums = jnp.concatenate([numerator, denominator], axis=0)
    sums = sums[:, :128] + sums[:, 128:]
    later = exchange(sums, tile1, r, [at_r(d) for d in (1, 2, 3)])
    later = exchange(later(), tile2, z, [at_z(d) for d in z_steps])

    here = pl.multiple_of(z * 32, 32)
    y_got = {}
    for s in (0, 1):
        for copy in z_in[s]:
            copy.wait_recv()
        total = part[s, pl.ds(here, 32), :]
        for d in z_steps:
            total = total + zbuf[s, (z + d + 8) % 8].astype(F32)
        ybuf[s, yhi] = total.astype(BF16)
        y_got[s] = [send(ybuf.at[s, yhi], ybuf.at[s, yhi], at_yhi(d)) for d in y_steps]
    later = exchange(later(), tile3, yhi, [at_yhi(d) for d in y_steps])
    last = []
    for s in (0, 1):
        for copy in y_got[s]:
            copy.wait_recv()
        total = ybuf[s, 0].astype(F32)
        for i in (1, 2, 3):
            total = total + ybuf[s, i].astype(F32)
        summed[s, pl.ds(here, 32), :] = total.astype(BF16)
        chunk = summed.at[s, pl.ds(here, 32), :]
        last += [send(chunk, chunk, at_z(d)) for d in z_steps]
    later = exchange(later(), tile4, x, [at_x(d) for d in x_steps])
    sums = later()
    rayleigh = jnp.sum(sums[:8]) / (jnp.sum(sums[8:]) + EPSILON)
    for copy in last:
        copy.wait_recv()
    for s in (0, 1):
        inside = (rows < block_rows[s]) & (columns < block_cols[s])
        live = own[s]
        full = jnp.where(inside, summed[s].astype(F32) + energy[s] * live, 0.0)
        sigma[s] = full.astype(BF16)
        residual[s] = (full - rayleigh * live).astype(BF16)
    copies.finish()


def per_device(wavefunction, energy, block_rows, block_cols, left_ops, right_ops, source, target):
    hbm = pl.BlockSpec(memory_space=pltpu.HBM)
    vmem = pl.BlockSpec(memory_space=pltpu.VMEM)
    block = jax.ShapeDtypeStruct((2, 256, 256), BF16)
    return pl.pallas_call(
        kernel,
        out_shape=(block, block),
        in_specs=[hbm] * 8,
        out_specs=(vmem, vmem),
        scratch_shapes=[pltpu.SMEM((4,), jnp.int32)] * 2
        + [pltpu.SMEM((2,), jnp.int32)] * 2
        + [pltpu.SMEM((2,), F32)]
        + [pltpu.VMEM((2, 1024, 256), BF16)] * 4
        + [
            pltpu.VMEM((4, 256, 1024), BF16),
            pltpu.VMEM((4, 256, 1024), BF16),
            pltpu.VMEM((4, 256, 256), F32),
            pltpu.VMEM((2, 256, 256), F32),
            pltpu.VMEM((2, 256, 256), BF16),
            pltpu.VMEM((2, 8, 32, 256), BF16),
            pltpu.VMEM((2, 4, 32, 256), BF16),
            pltpu.VMEM((2, 256, 256), BF16),
            pltpu.VMEM((2, 256, 256), F32),
            pltpu.VMEM((4, 16, 128), F32),
            pltpu.VMEM((8, 16, 128), F32),
            pltpu.VMEM((4, 16, 128), F32),
            pltpu.VMEM((4, 16, 128), F32),
            pltpu.SemaphoreType.DMA((8,)),
            pltpu.SemaphoreType.DMA((N_SEMS,)),
            pltpu.SemaphoreType.DMA((N_SEMS,)),
            pltpu.SemaphoreType.REGULAR((3,)),
        ],
        compiler_params=pltpu.CompilerParams(
            collective_id=0, has_side_effects=True, vmem_limit_bytes=VMEM_LIMIT
        ),
        name="sigma_step",
    )(source, target, block_rows, block_cols, energy, wavefunction, left_ops, right_ops)


def solution(mesh):
    in_specs = (
        P(None, "rows", "cols"),
        P(),
        P(),
        P(),
        P("terms", "rows", None),
        P("terms", "cols", None),
        P("terms"),
        P("terms"),
    )
    out_specs = (P(None, "rows", "cols"), P(None, "rows", "cols"))
    return jax.shard_map(per_device, mesh=mesh, in_specs=in_specs, out_specs=out_specs, check_vma=False)
```

```python
import functools

import jax
import jax.numpy as jnp
from jax import lax
from jax.experimental import pallas as pl
from jax.experimental.pallas import tpu as pltpu
from jax.sharding import PartitionSpec as P

MESH = pl.DeviceIdType.MESH
EPSILON = 1e-06
F32 = jnp.float32
BF16 = jnp.bfloat16
N_SEMS = 152
BATCHES = 4
BATCH_ROWS = 512 // BATCHES
CHUNK = BATCH_ROWS // 8
VMEM_LIMIT = 67043328


class Copies:
    def __init__(self, send_sems, recv_sems):
        self.send_sems, self.recv_sems, self.used, self.open = send_sems, recv_sems, 0, []

    def send(self, src, dst, device):
        at = self.used
        self.used += 1
        copy = pltpu.make_async_remote_copy(
            src, dst, self.send_sems.at[at], self.recv_sems.at[at], device_id=device, device_id_type=MESH
        )
        copy.start()
        self.open.append(copy)
        return copy

    def finish(self):
        for copy in self.open:
            copy.wait_send()


def kernel(
    source_in, target_in, rows_in, cols_in, energy_in, psi, left, right,
    summed, live_out, table,
    source, target, block_rows, block_cols, energy,
    own0, own1, own2, own3, far0, far1, far2, far3, half_products, lbuf, rbuf, adds, part, part_b, zbuf, ybuf,
    tile1, tile2, tile3, tile4, local_sems, send_sems, recv_sems, hello,
):
    t, r, x = lax.axis_index("terms"), lax.axis_index("rows"), lax.axis_index("cols")
    yhi, z, ylo, core = t // 8, t % 8, r // 2, r % 2
    parity = z % 2

    def at_y(dy):
        y = (yhi * 2 + ylo + dy + 8) % 8
        return {"terms": (y // 2) * 8 + z, "rows": (y % 2) * 2 + core}

    def at_z(dz):
        return {"terms": yhi * 8 + (z + dz + 8) % 8}

    def at_yhi(d):
        return {"terms": ((yhi + d + 4) % 4) * 8 + z}

    def at_x(dx):
        return {"cols": (x + dx + 4) % 4}

    def at_r(d):
        return {"rows": (r + d) % 4}

    partner = {"rows": ylo * 2 + 1 - core}
    z_steps = (4, 3, -3, 2, -2, 1, -1)
    y_steps = (2, 1, -1)
    x_steps = (1, -1, 2)

    def greet(sem, friends):
        for friend in friends:
            pl.semaphore_signal(sem, inc=1, device_id=friend, device_id_type=MESH)

    line = [at_y(1), at_y(-1), at_z(1), at_z(-1)]
    near = [partner, at_x(1), at_x(-1)] + line
    barrier = pltpu.get_barrier_semaphore()
    greet(barrier, near)

    owns = {0: own0, 1: own1, 2: own2, 3: own3}
    fars = {0: far0, 1: far1, 2: far2, 3: far3}
    mine = pl.multiple_of(core * 256, 256)
    tables = ((source_in, source), (target_in, target), (rows_in, block_rows), (cols_in, block_cols), (energy_in, energy))
    small = [pltpu.make_async_copy(a, b, local_sems.at[3 + i]) for i, (a, b) in enumerate(tables)]
    native = pltpu.make_async_copy(psi, own0.at[:, pl.ds(mine, 256), :], local_sems.at[0])
    native.start()
    for copy in small:
        copy.start()
    native.wait()
    pl.semaphore_wait(barrier, len(near))

    copies = Copies(send_sems, recv_sems)
    send = copies.send

    def unit(group, k, sector, half=None):
        if half is None:
            return group[k].at[sector, pl.ds(mine, 256), :]
        return group[k].at[sector, pl.ds(pl.multiple_of(mine + 128 * half, 128), 128), :]

    a_in = {1: [], 2: [], 3: []}
    b_in = {1: [], 2: [], 3: []}
    c_in = {1: [], 2: [], 3: []}
    d_in = {1: [], 2: [], 3: []}
    y_in = {0: [], 1: []}
    for half in (0, 1):
        piece = unit(owns, 0, parity, half)
        a_in[3].append(send(piece, unit(owns, 3, parity, half), at_x(1)))
        a_in[1].append(send(piece, unit(owns, 1, parity, half), at_x(-1)))
        y_in[0].append(send(unit(owns, 0, 0, half), unit(fars, 0, 0, half), at_y(1)))
        y_in[1].append(send(unit(owns, 0, 1, half), unit(fars, 0, 1, half), at_y(-1)))
    block = own0.at[:, pl.ds(mine, 256), :]
    own_in = {0: [send(block, block, partner)], 1: [], 2: [], 3: []}
    far_in = {0: [], 1: [], 2: [], 3: []}
    greet(hello.at[0], near)
    load_l = pltpu.make_async_copy(left, lbuf, local_sems.at[1])
    load_l.start()
    load_r = pltpu.make_async_copy(right, rbuf, local_sems.at[2])
    load_r.start()

    def share(arrivals, k, ref):
        arrivals[k].append(send(ref, ref, partner))

    def compute_own(k):
        for copy in own_in[k]:
            copy.wait_recv()
        depth = pl.multiple_of(ylo * 512, 512)

        for i in range(4):
            half_products[k, i] = jnp.dot(
                lbuf[i, :, pl.ds(depth, 512)], owns[k][source[i]], preferred_element_type=F32
            )

    def compute_far(k):
        for copy in far_in[k]:
            copy.wait_recv()
        depth = pl.multiple_of((1 - ylo) * 512, 512)
        start = pl.multiple_of(((x + k) % 4) * 256, 256)
        columns = lax.broadcasted_iota(jnp.int32, (256, 256), 1) + start

        for i in range(4):
            sector = source[i]
            product = half_products[k, i] + jnp.dot(
                lbuf[i, :, pl.ds(depth, 512)], fars[k][sector], preferred_element_type=F32
            )
            product = jnp.where(columns < block_cols[sector], product, 0.0).astype(BF16)
            added = lax.dot_general(
                product, rbuf[i, :, pl.ds(start, 256)], (((1,), (1,)), ((), ())), preferred_element_type=F32
            )
            adds[i] = added if k == 0 else adds[i] + added

    for copy in small:
        copy.wait()
    load_l.wait()
    depth_ids = lax.broadcasted_iota(jnp.int32, (256, 1024), 1)

    def mask_one(i, carry):
        lbuf[i] = jnp.where(depth_ids < block_rows[source[i]], lbuf[i], jnp.zeros((), BF16))
        return carry

    lax.fori_loop(0, 4, mask_one, 0)

    ways = (1, -1)
    for half, k in ((0, 3), (0, 1), (1, 1), (1, 3)):
        a_in[k][half].wait_recv()
        piece = unit(owns, k, parity, half)
        if (half, k) in ((0, 3), (1, 1)):
            a_in[2].append(send(piece, unit(owns, 2, parity, half), at_x(ways[half])))
        b_in[k].append(send(piece, piece, at_z(ways[half])))
    for k in (1, 3):
        share(own_in, k, unit(owns, k, parity))
    pl.semaphore_wait(hello.at[0], len(near))
    greet(hello.at[1], line)
    for half in (0, 1):
        for s in (0, 1):
            y_in[s][half].wait_recv()
        piece = unit(fars, 0, parity, half)
        c_in[3].append(send(piece, unit(fars, 3, parity, half), at_x(1)))
        c_in[1].append(send(piece, unit(fars, 1, parity, half), at_x(-1)))
    for s in (0, 1):
        share(far_in, 0, unit(fars, 0, s))
    for half in (0, 1):
        a_in[2][half].wait_recv()
        piece = unit(owns, 2, parity, half)
        c_in[2].append(send(piece, unit(fars, 2, parity, half), at_y(ways[half])))
        b_in[2].append(send(piece, piece, at_z(ways[half])))
    share(own_in, 2, unit(owns, 2, parity))
    compute_own(0)
    for half, k in ((0, 3), (0, 1), (1, 1), (1, 3)):
        b_in[k][half].wait_recv()
        d_in[k].append(send(unit(owns, k, 1 - parity, half), unit(fars, k, 1 - parity, half), at_y(ways[half])))
    for k in (1, 3):
        share(own_in, k, unit(owns, k, 1 - parity))
    pl.semaphore_wait(hello.at[1], len(line))
    greet(hello.at[2], line)
    for k in (1, 3):
        for half in (0, 1):
            c_in[k][half].wait_recv()
        share(far_in, k, unit(fars, k, parity))
    for half in (0, 1):
        c_in[2][half].wait_recv()
        piece = unit(fars, 2, parity, half)
        d_in[2].append(send(piece, piece, at_z(ways[half])))
    share(far_in, 2, unit(fars, 2, parity))
    for half in (0, 1):
        b_in[2][half].wait_recv()
    share(own_in, 2, unit(owns, 2, 1 - parity))
    load_r.wait()
    compute_far(0)
    compute_own(1)
    for k in (1, 3):
        for half in (0, 1):
            d_in[k][half].wait_recv()
        share(far_in, k, unit(fars, k, 1 - parity))
    compute_own(3)
    pl.semaphore_wait(hello.at[2], len(line))
    for half in (0, 1):
        d_in[2][half].wait_recv()
    share(far_in, 2, unit(fars, 2, 1 - parity))
    compute_own(2)
    compute_far(1)
    compute_far(3)
    compute_far(2)

    rows = lax.broadcasted_iota(jnp.int32, (256, 256), 0) + r * 256
    columns = lax.broadcasted_iota(jnp.int32, (256, 256), 1) + x * 256
    z_in = []
    for b in range(BATCHES):
        s, first = divmod(b * BATCH_ROWS, 256)
        span = slice(first, first + BATCH_ROWS)
        block = jnp.where(target[0] == s, adds[0, span, :], 0.0)
        for i in (1, 2, 3):
            block = block + jnp.where(target[i] == s, adds[i, span, :], 0.0)
        part[b] = block
        part_b[b] = block.astype(BF16)
        z_in.append([])
        for d in z_steps:
            there = pl.multiple_of(((z + d + 8) % 8) * CHUNK, CHUNK)
            z_in[b].append(send(part_b.at[b, pl.ds(there, CHUNK), :], zbuf.at[b, z], at_z(d)))
    numerator = jnp.zeros((8, 256), F32)
    denominator = jnp.zeros((8, 256), F32)
    for s in (0, 1):
        inside = (rows < block_rows[s]) & (columns < block_cols[s])
        live = jnp.where(inside, own0[s, pl.ds(mine, 256), :].astype(F32), 0.0)
        live_out[s] = live.astype(BF16)
        square = jnp.sum((live * live).reshape(32, 8, 256), axis=0) * (1.0 / 32)
        half = BATCHES // 2
        block = part[s * half : (s + 1) * half].reshape(256, 256)
        numerator += jnp.sum((live * block).reshape(32, 8, 256), axis=0) + energy[s] * square
        denominator += square

    def exchange(value, tiles, here, moves):
        tiles[here] = value
        got = [send(tiles.at[here], tiles.at[here], device) for device in moves]

        def total():
            for copy in got:
                copy.wait_recv()
            whole = tiles[0]
            for i in range(1, tiles.shape[0]):
                whole = whole + tiles[i]
            return whole

        return total

    sums = jnp.concatenate([numerator, denominator], axis=0)
    sums = sums[:, :128] + sums[:, 128:]
    later = exchange(sums, tile1, r, [at_r(d) for d in (1, 2, 3)])
    later = exchange(later(), tile2, z, [at_z(d) for d in z_steps])

    here = pl.multiple_of(z * CHUNK, CHUNK)
    chunk_rows = lax.broadcasted_iota(jnp.int32, (CHUNK, 256), 0) + (r * 256 + z * CHUNK)
    chunk_columns = lax.broadcasted_iota(jnp.int32, (CHUNK, 256), 1) + x * 256
    y_got, last = [], []

    def along_y(b):
        for copy in z_in[b]:
            copy.wait_recv()
        total = part[b, pl.ds(here, CHUNK), :]
        for d in z_steps:
            total = total + zbuf[b, (z + d + 8) % 8].astype(F32)
        ybuf[b, yhi] = total.astype(BF16)
        y_got.append([send(ybuf.at[b, yhi], ybuf.at[b, yhi], at_yhi(d)) for d in y_steps])

    def along_z(b):
        for copy in y_got[b]:
            copy.wait_recv()
        s, first = divmod(b * BATCH_ROWS, 256)
        total = ybuf[b, 0].astype(F32)
        for i in (1, 2, 3):
            total = total + ybuf[b, i].astype(F32)
        inside = (chunk_rows + first < block_rows[s]) & (chunk_columns < block_cols[s])
        at = pl.ds(pl.multiple_of(first + z * CHUNK, CHUNK), CHUNK)
        summed[s, at, :] = jnp.where(inside, total, 0.0).astype(BF16)
        chunk = summed.at[s, at, :]
        last.extend([send(chunk, chunk, at_z(d)) for d in z_steps])

    for b in range(BATCHES):
        along_y(b)
    later = exchange(later(), tile3, yhi, [at_yhi(d) for d in y_steps])
    for b in range(BATCHES):
        along_z(b)
    sums = exchange(later(), tile4, x, [at_x(d) for d in x_steps])()
    table[0:1, :] = jnp.full((1, 128), jnp.sum(sums[:8]) / (jnp.sum(sums[8:]) + EPSILON), F32)
    table[1:2, :] = jnp.full((1, 128), energy[0], F32)
    table[2:3, :] = jnp.full((1, 128), energy[1], F32)
    for copy in last:
        copy.wait_recv()
    copies.finish()


def finish_kernel(summed, live_in, table, sigma, residual):
    rayleigh = table[0:1, 0:1]
    for s in (0, 1):
        live = live_in[s].astype(F32)
        full = summed[s].astype(F32) + table[1 + s : 2 + s, 0:1] * live
        sigma[s] = full.astype(BF16)
        residual[s] = (full - rayleigh * live).astype(BF16)


def per_device(wavefunction, energy, block_rows, block_cols, left_ops, right_ops, source, target):
    hbm = pl.BlockSpec(memory_space=pltpu.HBM)
    vmem = pl.BlockSpec(memory_space=pltpu.VMEM)
    block = jax.ShapeDtypeStruct((2, 256, 256), BF16)
    parts = pl.pallas_call(
        kernel,
        out_shape=(block, block, jax.ShapeDtypeStruct((8, 128), F32)),
        in_specs=[hbm] * 8,
        out_specs=(vmem, vmem, vmem),
        scratch_shapes=[pltpu.SMEM((4,), jnp.int32)] * 2
        + [pltpu.SMEM((2,), jnp.int32)] * 2
        + [pltpu.SMEM((2,), F32)]
        + [pltpu.VMEM((2, 512, 256), BF16)] * 8
        + [pltpu.VMEM((4, 4, 256, 256), F32)]
        + [
            pltpu.VMEM((4, 256, 1024), BF16),
            pltpu.VMEM((4, 256, 1024), BF16),
            pltpu.VMEM((4, 256, 256), F32),
            pltpu.VMEM((BATCHES, BATCH_ROWS, 256), F32),
            pltpu.VMEM((BATCHES, BATCH_ROWS, 256), BF16),
            pltpu.VMEM((BATCHES, 8, CHUNK, 256), BF16),
            pltpu.VMEM((BATCHES, 4, CHUNK, 256), BF16),
            pltpu.VMEM((4, 16, 128), F32),
            pltpu.VMEM((8, 16, 128), F32),
            pltpu.VMEM((4, 16, 128), F32),
            pltpu.VMEM((4, 16, 128), F32),
            pltpu.SemaphoreType.DMA((8,)),
            pltpu.SemaphoreType.DMA((N_SEMS,)),
            pltpu.SemaphoreType.DMA((N_SEMS,)),
            pltpu.SemaphoreType.REGULAR((3,)),
        ],
        compiler_params=pltpu.CompilerParams(
            collective_id=0, has_side_effects=True, vmem_limit_bytes=VMEM_LIMIT
        ),
        name="sigma_step",
    )(source, target, block_rows, block_cols, energy, wavefunction, left_ops, right_ops)
    return pl.pallas_call(
        finish_kernel,
        out_shape=(block, block),
        in_specs=[vmem] * 3,
        out_specs=(vmem, vmem),
        name="sigma_and_residual",
    )(*parts)


def solution(mesh):
    in_specs = (
        P(None, "rows", "cols"),
        P(),
        P(),
        P(),
        P("terms", "rows", None),
        P("terms", "cols", None),
        P("terms"),
        P("terms"),
    )
    out_specs = (P(None, "rows", "cols"), P(None, "rows", "cols"))
    return jax.shard_map(per_device, mesh=mesh, in_specs=in_specs, out_specs=out_specs, check_vma=False)
```

```python
import functools

import jax
import jax.numpy as jnp
from jax import lax
from jax.experimental import pallas as pl
from jax.experimental.pallas import tpu as pltpu
from jax.sharding import PartitionSpec as P

MESH = pl.DeviceIdType.MESH
EPSILON = 1e-06
F32 = jnp.float32
BF16 = jnp.bfloat16
N_SEMS = 160
BATCHES = 4
BATCH_ROWS = 512 // BATCHES
CHUNK = BATCH_ROWS // 8
VMEM_LIMIT = 67043328


class Copies:
    def __init__(self, send_sems, recv_sems):
        self.send_sems, self.recv_sems, self.used, self.open = send_sems, recv_sems, 0, []

    def send(self, src, dst, device):
        at = self.used
        self.used += 1
        copy = pltpu.make_async_remote_copy(
            src, dst, self.send_sems.at[at], self.recv_sems.at[at], device_id=device, device_id_type=MESH
        )
        copy.start()
        self.open.append(copy)
        return copy

    def finish(self):
        for copy in self.open:
            copy.wait_send()


def kernel(
    source_in, target_in, rows_in, cols_in, energy_in, psi, left, right,
    summed, live_out, table,
    source, target, block_rows, block_cols, energy,
    own0, own1, own2, own3, far0, far1, far2, far3, half_products, lbuf, rbuf, adds, part, part_b, zbuf, ybuf,
    tile1, tile2, tile3, tile4, local_sems, send_sems, recv_sems, hello,
):
    t, r, x = lax.axis_index("terms"), lax.axis_index("rows"), lax.axis_index("cols")
    yhi, z, ylo, core = t // 8, t % 8, r // 2, r % 2
    parity = z % 2

    def at_y(dy):
        y = (yhi * 2 + ylo + dy + 8) % 8
        return {"terms": (y // 2) * 8 + z, "rows": (y % 2) * 2 + core}

    def at_z(dz):
        return {"terms": yhi * 8 + (z + dz + 8) % 8}

    def at_yhi(d):
        return {"terms": ((yhi + d + 4) % 4) * 8 + z}

    def at_corner(way):
        y = (yhi * 2 + ylo + way + 8) % 8
        return {"terms": (y // 2) * 8 + (z + way + 8) % 8, "rows": (y % 2) * 2 + core}

    def at_x(dx):
        return {"cols": (x + dx + 4) % 4}

    def at_r(d):
        return {"rows": (r + d) % 4}

    partner = {"rows": ylo * 2 + 1 - core}
    z_steps = (4, 3, -3, 2, -2, 1, -1)
    y_steps = (2, 1, -1)
    x_steps = (1, -1, 2)

    def greet(sem, friends):
        for friend in friends:
            pl.semaphore_signal(sem, inc=1, device_id=friend, device_id_type=MESH)

    line = [at_y(1), at_y(-1), at_z(1), at_z(-1)]
    near = [partner, at_x(1), at_x(-1)] + line
    barrier = pltpu.get_barrier_semaphore()
    greet(barrier, near)

    owns = {0: own0, 1: own1, 2: own2, 3: own3}
    fars = {0: far0, 1: far1, 2: far2, 3: far3}
    mine = pl.multiple_of(core * 256, 256)
    tables = ((source_in, source), (target_in, target), (rows_in, block_rows), (cols_in, block_cols), (energy_in, energy))
    small = [pltpu.make_async_copy(a, b, local_sems.at[3 + i]) for i, (a, b) in enumerate(tables)]
    native = pltpu.make_async_copy(psi, own0.at[:, pl.ds(mine, 256), :], local_sems.at[0])
    native.start()
    for copy in small:
        copy.start()
    native.wait()
    pl.semaphore_wait(barrier, len(near))

    copies = Copies(send_sems, recv_sems)
    send = copies.send

    def unit(group, k, sector, piece=0, pieces=1):
        size = 256 // pieces
        return group[k].at[sector, pl.ds(pl.multiple_of(mine + size * piece, size), size), :]

    a_in = {1: [], 2: [], 3: []}
    b_in = {1: [], 2: [], 3: []}
    c_in = {1: [], 2: [], 3: []}
    d_in = {1: [], 2: [], 3: []}
    y_in = {0: [], 1: []}
    block = own0.at[:, pl.ds(mine, 256), :]
    own_in = {0: [send(block, block, partner)], 1: [], 2: [], 3: []}
    far_in = {0: [], 1: [], 2: [], 3: []}
    for q in (0, 1):
        piece = unit(owns, 0, parity, q, 2)
        a_in[3].append(send(piece, unit(owns, 3, parity, q, 2), at_x(1)))
        a_in[1].append(send(piece, unit(owns, 1, parity, q, 2), at_x(-1)))
        y_in[0].append(send(unit(owns, 0, 0, q, 2), unit(fars, 0, 0, q, 2), at_y(1)))
        y_in[1].append(send(unit(owns, 0, 1, q, 2), unit(fars, 0, 1, q, 2), at_y(-1)))
    greet(hello.at[0], near)
    load_l = pltpu.make_async_copy(left, lbuf, local_sems.at[1])
    load_l.start()
    load_r = pltpu.make_async_copy(right, rbuf, local_sems.at[2])
    load_r.start()

    def share(arrivals, k, ref):
        arrivals[k].append(send(ref, ref, partner))

    def compute_own(k):
        for copy in own_in[k]:
            copy.wait_recv()
        depth = pl.multiple_of(ylo * 512, 512)

        for i in range(4):
            half_products[k, i] = jnp.dot(
                lbuf[i, :, pl.ds(depth, 512)], owns[k][source[i]], preferred_element_type=F32
            )

    def compute_far(k):
        for copy in far_in[k]:
            copy.wait_recv()
        depth = pl.multiple_of((1 - ylo) * 512, 512)
        start = pl.multiple_of(((x + k) % 4) * 256, 256)
        columns = lax.broadcasted_iota(jnp.int32, (256, 256), 1) + start

        for i in range(4):
            sector = source[i]
            product = half_products[k, i] + jnp.dot(
                lbuf[i, :, pl.ds(depth, 512)], fars[k][sector], preferred_element_type=F32
            )
            product = jnp.where(columns < block_cols[sector], product, 0.0).astype(BF16)
            added = lax.dot_general(
                product, rbuf[i, :, pl.ds(start, 256)], (((1,), (1,)), ((), ())), preferred_element_type=F32
            )
            adds[i] = added if k == 0 else adds[i] + added

    for copy in small:
        copy.wait()
    load_l.wait()
    depth_ids = lax.broadcasted_iota(jnp.int32, (256, 1024), 1)

    def mask_one(i, carry):
        lbuf[i] = jnp.where(depth_ids < block_rows[source[i]], lbuf[i], jnp.zeros((), BF16))
        return carry

    lax.fori_loop(0, 4, mask_one, 0)

    compute_own(0)
    ways = (1, -1)
    for q in (0, 1):
        for k in (1, 3):
            a_in[k][q].wait_recv()
            piece = unit(owns, k, parity, q, 2)
            b_in[k].append(send(piece, piece, at_z(ways[q])))
            if k == (3, 1)[q]:
                a_in[2].append(send(piece, unit(owns, 2, parity, q, 2), at_x(ways[q])))
            share(own_in, k, piece)
    pl.semaphore_wait(hello.at[0], len(near))
    greet(hello.at[1], line)
    for q in (0, 1):
        for s in (0, 1):
            y_in[s][q].wait_recv()
        piece = unit(fars, 0, parity, q, 2)
        c_in[1].append(send(piece, unit(fars, 1, parity, q, 2), at_x(-1)))
        c_in[3].append(send(piece, unit(fars, 3, parity, q, 2), at_x(1)))
        for s in (0, 1):
            share(far_in, 0, unit(fars, 0, s, q, 2))

    def corner_rows(k):
        for q in (0, 1):
            b_in[k][q].wait_recv()
            piece, there = unit(owns, k, 1 - parity, q, 2), unit(fars, k, 1 - parity, q, 2)
            d_in[k].append(send(piece, there, at_y(ways[q])))
            share(own_in, k, piece)

    def pass_to_partner(arrived, arrivals, group, k, sector):
        for q in (0, 1):
            arrived[k][q].wait_recv()
            share(arrivals, k, unit(group, k, sector, q, 2))

    corner_rows(1)
    for q in (0, 1):
        a_in[2][q].wait_recv()
        piece, there = unit(owns, 2, parity, q, 2), unit(fars, 2, parity, q, 2)
        b_in[2].append(send(piece, piece, at_z(ways[q])))
        d_in[2].append(send(piece, there, at_corner(ways[q])))
        c_in[2].append(send(piece, there, at_y(ways[q])))
        share(own_in, 2, piece)
    corner_rows(3)
    pl.semaphore_wait(hello.at[1], len(line))
    greet(hello.at[2], line)
    load_r.wait()
    compute_far(0)
    pass_to_partner(c_in, far_in, fars, 1, parity)
    pass_to_partner(d_in, far_in, fars, 1, 1 - parity)
    pass_to_partner(c_in, far_in, fars, 3, parity)
    compute_own(1)
    compute_far(1)
    pass_to_partner(b_in, own_in, owns, 2, 1 - parity)
    pass_to_partner(c_in, far_in, fars, 2, parity)
    pass_to_partner(d_in, far_in, fars, 3, 1 - parity)
    pass_to_partner(d_in, far_in, fars, 2, 1 - parity)
    compute_own(3)
    compute_own(2)
    pl.semaphore_wait(hello.at[2], len(line))
    compute_far(3)
    compute_far(2)

    rows = lax.broadcasted_iota(jnp.int32, (256, 256), 0) + r * 256
    columns = lax.broadcasted_iota(jnp.int32, (256, 256), 1) + x * 256
    z_in = []
    for b in range(BATCHES):
        s, first = divmod(b * BATCH_ROWS, 256)
        span = slice(first, first + BATCH_ROWS)
        block = jnp.where(target[0] == s, adds[0, span, :], 0.0)
        for i in (1, 2, 3):
            block = block + jnp.where(target[i] == s, adds[i, span, :], 0.0)
        part[b] = block
        part_b[b] = block.astype(BF16)
        z_in.append([])
        for d in z_steps:
            there = pl.multiple_of(((z + d + 8) % 8) * CHUNK, CHUNK)
            z_in[b].append(send(part_b.at[b, pl.ds(there, CHUNK), :], zbuf.at[b, z], at_z(d)))
    numerator = jnp.zeros((8, 256), F32)
    denominator = jnp.zeros((8, 256), F32)
    for s in (0, 1):
        inside = (rows < block_rows[s]) & (columns < block_cols[s])
        live = jnp.where(inside, own0[s, pl.ds(mine, 256), :].astype(F32), 0.0)
        live_out[s] = live.astype(BF16)
        square = jnp.sum((live * live).reshape(32, 8, 256), axis=0) * (1.0 / 32)
        half = BATCHES // 2
        block = part[s * half : (s + 1) * half].reshape(256, 256)
        numerator += jnp.sum((live * block).reshape(32, 8, 256), axis=0) + energy[s] * square
        denominator += square

    def exchange(value, tiles, here, moves):
        tiles[here] = value
        got = [send(tiles.at[here], tiles.at[here], device) for device in moves]

        def total():
            for copy in got:
                copy.wait_recv()
            whole = tiles[0]
            for i in range(1, tiles.shape[0]):
                whole = whole + tiles[i]
            return whole

        return total

    sums = jnp.concatenate([numerator, denominator], axis=0)
    sums = sums[:, :128] + sums[:, 128:]
    later = exchange(sums, tile1, r, [at_r(d) for d in (1, 2, 3)])
    later = exchange(later(), tile2, z, [at_z(d) for d in z_steps])

    here = pl.multiple_of(z * CHUNK, CHUNK)
    chunk_rows = lax.broadcasted_iota(jnp.int32, (CHUNK, 256), 0) + (r * 256 + z * CHUNK)
    chunk_columns = lax.broadcasted_iota(jnp.int32, (CHUNK, 256), 1) + x * 256
    y_got, last = [], []

    def along_y(b):
        for copy in z_in[b]:
            copy.wait_recv()
        total = part[b, pl.ds(here, CHUNK), :]
        for d in z_steps:
            total = total + zbuf[b, (z + d + 8) % 8].astype(F32)
        ybuf[b, yhi] = total.astype(BF16)
        y_got.append([send(ybuf.at[b, yhi], ybuf.at[b, yhi], at_yhi(d)) for d in y_steps])

    def along_z(b):
        for copy in y_got[b]:
            copy.wait_recv()
        s, first = divmod(b * BATCH_ROWS, 256)
        total = ybuf[b, 0].astype(F32)
        for i in (1, 2, 3):
            total = total + ybuf[b, i].astype(F32)
        inside = (chunk_rows + first < block_rows[s]) & (chunk_columns < block_cols[s])
        at = pl.ds(pl.multiple_of(first + z * CHUNK, CHUNK), CHUNK)
        summed[s, at, :] = jnp.where(inside, total, 0.0).astype(BF16)
        chunk = summed.at[s, at, :]
        last.extend([send(chunk, chunk, at_z(d)) for d in z_steps])

    for b in range(BATCHES):
        along_y(b)
    later = exchange(later(), tile3, yhi, [at_yhi(d) for d in y_steps])
    for b in range(BATCHES):
        along_z(b)
    sums = exchange(later(), tile4, x, [at_x(d) for d in x_steps])()
    table[0:1, :] = jnp.full((1, 128), jnp.sum(sums[:8]) / (jnp.sum(sums[8:]) + EPSILON), F32)
    table[1:2, :] = jnp.full((1, 128), energy[0], F32)
    table[2:3, :] = jnp.full((1, 128), energy[1], F32)
    for copy in last:
        copy.wait_recv()
    copies.finish()


def finish_kernel(summed, live_in, table, sigma, residual):
    rayleigh = table[0:1, 0:1]
    for s in (0, 1):
        live = live_in[s].astype(F32)
        full = summed[s].astype(F32) + table[1 + s : 2 + s, 0:1] * live
        sigma[s] = full.astype(BF16)
        residual[s] = (full - rayleigh * live).astype(BF16)


def per_device(wavefunction, energy, block_rows, block_cols, left_ops, right_ops, source, target):
    hbm = pl.BlockSpec(memory_space=pltpu.HBM)
    vmem = pl.BlockSpec(memory_space=pltpu.VMEM)
    block = jax.ShapeDtypeStruct((2, 256, 256), BF16)
    parts = pl.pallas_call(
        kernel,
        out_shape=(block, block, jax.ShapeDtypeStruct((8, 128), F32)),
        in_specs=[hbm] * 8,
        out_specs=(vmem, vmem, vmem),
        scratch_shapes=[pltpu.SMEM((4,), jnp.int32)] * 2
        + [pltpu.SMEM((2,), jnp.int32)] * 2
        + [pltpu.SMEM((2,), F32)]
        + [pltpu.VMEM((2, 512, 256), BF16)] * 8
        + [pltpu.VMEM((4, 4, 256, 256), F32)]
        + [
            pltpu.VMEM((4, 256, 1024), BF16),
            pltpu.VMEM((4, 256, 1024), BF16),
            pltpu.VMEM((4, 256, 256), F32),
            pltpu.VMEM((BATCHES, BATCH_ROWS, 256), F32),
            pltpu.VMEM((BATCHES, BATCH_ROWS, 256), BF16),
            pltpu.VMEM((BATCHES, 8, CHUNK, 256), BF16),
            pltpu.VMEM((BATCHES, 4, CHUNK, 256), BF16),
            pltpu.VMEM((4, 16, 128), F32),
            pltpu.VMEM((8, 16, 128), F32),
            pltpu.VMEM((4, 16, 128), F32),
            pltpu.VMEM((4, 16, 128), F32),
            pltpu.SemaphoreType.DMA((8,)),
            pltpu.SemaphoreType.DMA((N_SEMS,)),
            pltpu.SemaphoreType.DMA((N_SEMS,)),
            pltpu.SemaphoreType.REGULAR((3,)),
        ],
        compiler_params=pltpu.CompilerParams(
            collective_id=0, has_side_effects=True, vmem_limit_bytes=VMEM_LIMIT
        ),
        name="sigma_step",
    )(source, target, block_rows, block_cols, energy, wavefunction, left_ops, right_ops)
    return pl.pallas_call(
        finish_kernel,
        out_shape=(block, block),
        in_specs=[vmem] * 3,
        out_specs=(vmem, vmem),
        name="sigma_and_residual",
    )(*parts)


def solution(mesh):
    in_specs = (
        P(None, "rows", "cols"),
        P(),
        P(),
        P(),
        P("terms", "rows", None),
        P("terms", "cols", None),
        P("terms"),
        P("terms"),
    )
    out_specs = (P(None, "rows", "cols"), P(None, "rows", "cols"))
    return jax.shard_map(per_device, mesh=mesh, in_specs=in_specs, out_specs=out_specs, check_vma=False)
```

```python
import functools

import jax
import jax.numpy as jnp
from jax import lax
from jax.experimental import pallas as pl
from jax.experimental.pallas import tpu as pltpu
from jax.sharding import PartitionSpec as P

MESH = pl.DeviceIdType.MESH
EPSILON = 1e-06
F32 = jnp.float32
BF16 = jnp.bfloat16
N_SEMS = 160
BATCHES = 4
BATCH_ROWS = 512 // BATCHES
CHUNK = BATCH_ROWS // 8
VMEM_LIMIT = 67043328


class Copies:
    def __init__(self, send_sems, recv_sems):
        self.send_sems, self.recv_sems, self.used, self.open = send_sems, recv_sems, 0, []

    def send(self, src, dst, device):
        at = self.used
        self.used += 1
        copy = pltpu.make_async_remote_copy(
            src, dst, self.send_sems.at[at], self.recv_sems.at[at], device_id=device, device_id_type=MESH
        )
        copy.start()
        self.open.append(copy)
        return copy

    def finish(self):
        for copy in self.open:
            copy.wait_send()


def kernel(
    source_in, target_in, rows_in, cols_in, energy_in, psi, left, right,
    summed, live_out, table,
    source, target, block_rows, block_cols, energy,
    own0, own1, own2, own3, far0, far1, far2, far3, half_products, lbuf, rbuf, adds, part, part_b, zbuf, ybuf,
    tile1, tile2, tile3, tile4, local_sems, send_sems, recv_sems, hello,
):
    t, r, x = lax.axis_index("terms"), lax.axis_index("rows"), lax.axis_index("cols")
    yhi, z, ylo, core = t // 8, t % 8, r // 2, r % 2
    parity = z % 2

    def at_y(dy):
        y = (yhi * 2 + ylo + dy + 8) % 8
        return {"terms": (y // 2) * 8 + z, "rows": (y % 2) * 2 + core}

    def at_z(dz):
        return {"terms": yhi * 8 + (z + dz + 8) % 8}

    def at_yhi(d):
        return {"terms": ((yhi + d + 4) % 4) * 8 + z}

    def at_corner(way):
        y = (yhi * 2 + ylo + way + 8) % 8
        return {"terms": (y // 2) * 8 + (z + way + 8) % 8, "rows": (y % 2) * 2 + core}

    def at_x(dx):
        return {"cols": (x + dx + 4) % 4}

    def at_r(d):
        return {"rows": (r + d) % 4}

    partner = {"rows": ylo * 2 + 1 - core}
    z_steps = (4, 3, -3, 2, -2, 1, -1)
    y_steps = (2, 1, -1)
    x_steps = (1, -1, 2)

    def greet(sem, friends):
        for friend in friends:
            pl.semaphore_signal(sem, inc=1, device_id=friend, device_id_type=MESH)

    line = [at_y(1), at_y(-1), at_z(1), at_z(-1)]
    near = [partner, at_x(1), at_x(-1)] + line
    barrier = pltpu.get_barrier_semaphore()
    greet(barrier, near)

    owns = {0: own0, 1: own1, 2: own2, 3: own3}
    fars = {0: far0, 1: far1, 2: far2, 3: far3}
    mine = pl.multiple_of(core * 256, 256)
    tables = ((source_in, source), (target_in, target), (rows_in, block_rows), (cols_in, block_cols), (energy_in, energy))
    small = [pltpu.make_async_copy(a, b, local_sems.at[3 + i]) for i, (a, b) in enumerate(tables)]
    native = pltpu.make_async_copy(psi, own0.at[:, pl.ds(mine, 256), :], local_sems.at[0])
    native.start()
    for copy in small:
        copy.start()
    load_l = pltpu.make_async_copy(left, lbuf, local_sems.at[1])
    load_l.start()
    native.wait()
    pl.semaphore_wait(barrier, len(near))

    copies = Copies(send_sems, recv_sems)
    send = copies.send

    def unit(group, k, sector, piece=0, pieces=1):
        size = 256 // pieces
        return group[k].at[sector, pl.ds(pl.multiple_of(mine + size * piece, size), size), :]

    a_in = {1: [], 2: [], 3: []}
    b_in = {1: [], 2: [], 3: []}
    c_in = {1: [], 2: [], 3: []}
    d_in = {1: [], 2: [], 3: []}
    y_in = {0: [], 1: []}
    block = own0.at[:, pl.ds(mine, 256), :]
    own_in = {0: [send(block, block, partner)], 1: [], 2: [], 3: []}
    far_in = {0: [], 1: [], 2: [], 3: []}
    for q in (0, 1):
        piece = unit(owns, 0, parity, q, 2)
        a_in[3].append(send(piece, unit(owns, 3, parity, q, 2), at_x(1)))
        a_in[1].append(send(piece, unit(owns, 1, parity, q, 2), at_x(-1)))
        y_in[0].append(send(unit(owns, 0, 0, q, 2), unit(fars, 0, 0, q, 2), at_y(1)))
        y_in[1].append(send(unit(owns, 0, 1, q, 2), unit(fars, 0, 1, q, 2), at_y(-1)))
    greet(hello.at[0], near)
    load_r = pltpu.make_async_copy(right, rbuf, local_sems.at[2])
    load_r.start()

    def share(arrivals, k, ref):
        arrivals[k].append(send(ref, ref, partner))

    def compute_own(k):
        for copy in own_in[k]:
            copy.wait_recv()
        depth = pl.multiple_of(ylo * 512, 512)

        for i in range(4):
            half_products[k, i] = jnp.dot(
                lbuf[i, :, pl.ds(depth, 512)], owns[k][source[i]], preferred_element_type=F32
            )

    def compute_far(k):
        for copy in far_in[k]:
            copy.wait_recv()
        depth = pl.multiple_of((1 - ylo) * 512, 512)
        start = pl.multiple_of(((x + k) % 4) * 256, 256)
        columns = lax.broadcasted_iota(jnp.int32, (256, 256), 1) + start

        for i in range(4):
            sector = source[i]
            product = half_products[k, i] + jnp.dot(
                lbuf[i, :, pl.ds(depth, 512)], fars[k][sector], preferred_element_type=F32
            )
            product = jnp.where(columns < block_cols[sector], product, 0.0).astype(BF16)
            added = lax.dot_general(
                product, rbuf[i, :, pl.ds(start, 256)], (((1,), (1,)), ((), ())), preferred_element_type=F32
            )
            adds[i] = added if k == 0 else adds[i] + added

    for copy in small:
        copy.wait()
    load_l.wait()
    depth_ids = lax.broadcasted_iota(jnp.int32, (256, 1024), 1)

    def mask_one(i, carry):
        lbuf[i] = jnp.where(depth_ids < block_rows[source[i]], lbuf[i], jnp.zeros((), BF16))
        return carry

    lax.fori_loop(0, 4, mask_one, 0)

    compute_own(0)
    ways = (1, -1)
    for q in (0, 1):
        for k in (1, 3):
            a_in[k][q].wait_recv()
            piece = unit(owns, k, parity, q, 2)
            b_in[k].append(send(piece, piece, at_z(ways[q])))
            if k == (3, 1)[q]:
                a_in[2].append(send(piece, unit(owns, 2, parity, q, 2), at_x(ways[q])))
            share(own_in, k, piece)
    pl.semaphore_wait(hello.at[0], len(near))
    greet(hello.at[1], line)
    for q in (0, 1):
        for s in (0, 1):
            y_in[s][q].wait_recv()
        piece = unit(fars, 0, parity, q, 2)
        c_in[1].append(send(piece, unit(fars, 1, parity, q, 2), at_x(-1)))
        c_in[3].append(send(piece, unit(fars, 3, parity, q, 2), at_x(1)))
        for s in (0, 1):
            share(far_in, 0, unit(fars, 0, s, q, 2))

    def corner_rows(k):
        for q in (0, 1):
            b_in[k][q].wait_recv()
            piece, there = unit(owns, k, 1 - parity, q, 2), unit(fars, k, 1 - parity, q, 2)
            d_in[k].append(send(piece, there, at_y(ways[q])))
            share(own_in, k, piece)

    def pass_to_partner(arrived, arrivals, group, k, sector):
        for q in (0, 1):
            arrived[k][q].wait_recv()
            share(arrivals, k, unit(group, k, sector, q, 2))

    corner_rows(1)
    for q in (0, 1):
        a_in[2][q].wait_recv()
        piece, there = unit(owns, 2, parity, q, 2), unit(fars, 2, parity, q, 2)
        b_in[2].append(send(piece, piece, at_z(ways[q])))
        d_in[2].append(send(piece, there, at_corner(ways[q])))
        c_in[2].append(send(piece, there, at_y(ways[q])))
        share(own_in, 2, piece)
    corner_rows(3)
    pl.semaphore_wait(hello.at[1], len(line))
    greet(hello.at[2], line)
    load_r.wait()
    compute_far(0)
    pass_to_partner(c_in, far_in, fars, 1, parity)
    pass_to_partner(d_in, far_in, fars, 1, 1 - parity)
    pass_to_partner(c_in, far_in, fars, 3, parity)
    compute_own(1)
    compute_far(1)
    pass_to_partner(b_in, own_in, owns, 2, 1 - parity)
    pass_to_partner(c_in, far_in, fars, 2, parity)
    pass_to_partner(d_in, far_in, fars, 3, 1 - parity)
    pass_to_partner(d_in, far_in, fars, 2, 1 - parity)
    compute_own(3)
    compute_own(2)
    pl.semaphore_wait(hello.at[2], len(line))
    compute_far(3)
    compute_far(2)

    rows = lax.broadcasted_iota(jnp.int32, (256, 256), 0) + r * 256
    columns = lax.broadcasted_iota(jnp.int32, (256, 256), 1) + x * 256
    z_in = []
    for b in range(BATCHES):
        s, first = divmod(b * BATCH_ROWS, 256)
        span = slice(first, first + BATCH_ROWS)
        block = jnp.where(target[0] == s, adds[0, span, :], 0.0)
        for i in (1, 2, 3):
            block = block + jnp.where(target[i] == s, adds[i, span, :], 0.0)
        part[b] = block
        part_b[b] = block.astype(BF16)
        z_in.append([])
        for d in z_steps:
            there = pl.multiple_of(((z + d + 8) % 8) * CHUNK, CHUNK)
            z_in[b].append(send(part_b.at[b, pl.ds(there, CHUNK), :], zbuf.at[b, z], at_z(d)))
    numerator = jnp.zeros((8, 256), F32)
    denominator = jnp.zeros((8, 256), F32)
    for s in (0, 1):
        inside = (rows < block_rows[s]) & (columns < block_cols[s])
        live = jnp.where(inside, own0[s, pl.ds(mine, 256), :].astype(F32), 0.0)
        live_out[s] = live.astype(BF16)
        square = jnp.sum((live * live).reshape(32, 8, 256), axis=0) * (1.0 / 32)
        half = BATCHES // 2
        block = part[s * half : (s + 1) * half].reshape(256, 256)
        numerator += jnp.sum((live * block).reshape(32, 8, 256), axis=0) + energy[s] * square
        denominator += square

    def exchange(value, tiles, here, moves):
        tiles[here] = value
        got = [send(tiles.at[here], tiles.at[here], device) for device in moves]

        def total():
            for copy in got:
                copy.wait_recv()
            whole = tiles[0]
            for i in range(1, tiles.shape[0]):
                whole = whole + tiles[i]
            return whole

        return total

    sums = jnp.concatenate([numerator, denominator], axis=0)
    sums = sums[:, :128] + sums[:, 128:]
    later = exchange(sums, tile1, r, [at_r(d) for d in (1, 2, 3)])
    later = exchange(later(), tile2, z, [at_z(d) for d in z_steps])

    here = pl.multiple_of(z * CHUNK, CHUNK)
    chunk_rows = lax.broadcasted_iota(jnp.int32, (CHUNK, 256), 0) + (r * 256 + z * CHUNK)
    chunk_columns = lax.broadcasted_iota(jnp.int32, (CHUNK, 256), 1) + x * 256
    y_got, last = [], []

    def along_y(b):
        for copy in z_in[b]:
            copy.wait_recv()
        total = part[b, pl.ds(here, CHUNK), :]
        for d in z_steps:
            total = total + zbuf[b, (z + d + 8) % 8].astype(F32)
        ybuf[b, yhi] = total.astype(BF16)
        y_got.append([send(ybuf.at[b, yhi], ybuf.at[b, yhi], at_yhi(d)) for d in y_steps])

    def along_z(b):
        for copy in y_got[b]:
            copy.wait_recv()
        s, first = divmod(b * BATCH_ROWS, 256)
        total = ybuf[b, 0].astype(F32)
        for i in (1, 2, 3):
            total = total + ybuf[b, i].astype(F32)
        inside = (chunk_rows + first < block_rows[s]) & (chunk_columns < block_cols[s])
        at = pl.ds(pl.multiple_of(first + z * CHUNK, CHUNK), CHUNK)
        summed[s, at, :] = jnp.where(inside, total, 0.0).astype(BF16)
        chunk = summed.at[s, at, :]
        last.extend([send(chunk, chunk, at_z(d)) for d in z_steps])

    for b in range(BATCHES):
        along_y(b)
    later = exchange(later(), tile3, yhi, [at_yhi(d) for d in y_steps])
    for b in range(BATCHES):
        along_z(b)
    sums = exchange(later(), tile4, x, [at_x(d) for d in x_steps])()
    table[0:1, :] = jnp.full((1, 128), jnp.sum(sums[:8]) / (jnp.sum(sums[8:]) + EPSILON), F32)
    table[1:2, :] = jnp.full((1, 128), energy[0], F32)
    table[2:3, :] = jnp.full((1, 128), energy[1], F32)
    for copy in last:
        copy.wait_recv()
    copies.finish()


def finish_kernel(summed, live_in, table, sigma, residual):
    rayleigh = table[0:1, 0:1]
    for s in (0, 1):
        live = live_in[s].astype(F32)
        full = summed[s].astype(F32) + table[1 + s : 2 + s, 0:1] * live
        sigma[s] = full.astype(BF16)
        residual[s] = (full - rayleigh * live).astype(BF16)


def per_device(wavefunction, energy, block_rows, block_cols, left_ops, right_ops, source, target):
    hbm = pl.BlockSpec(memory_space=pltpu.HBM)
    vmem = pl.BlockSpec(memory_space=pltpu.VMEM)
    block = jax.ShapeDtypeStruct((2, 256, 256), BF16)
    parts = pl.pallas_call(
        kernel,
        out_shape=(block, block, jax.ShapeDtypeStruct((8, 128), F32)),
        in_specs=[hbm] * 8,
        out_specs=(vmem, vmem, vmem),
        scratch_shapes=[pltpu.SMEM((4,), jnp.int32)] * 2
        + [pltpu.SMEM((2,), jnp.int32)] * 2
        + [pltpu.SMEM((2,), F32)]
        + [pltpu.VMEM((2, 512, 256), BF16)] * 8
        + [pltpu.VMEM((4, 4, 256, 256), F32)]
        + [
            pltpu.VMEM((4, 256, 1024), BF16),
            pltpu.VMEM((4, 256, 1024), BF16),
            pltpu.VMEM((4, 256, 256), F32),
            pltpu.VMEM((BATCHES, BATCH_ROWS, 256), F32),
            pltpu.VMEM((BATCHES, BATCH_ROWS, 256), BF16),
            pltpu.VMEM((BATCHES, 8, CHUNK, 256), BF16),
            pltpu.VMEM((BATCHES, 4, CHUNK, 256), BF16),
            pltpu.VMEM((4, 16, 128), F32),
            pltpu.VMEM((8, 16, 128), F32),
            pltpu.VMEM((4, 16, 128), F32),
            pltpu.VMEM((4, 16, 128), F32),
            pltpu.SemaphoreType.DMA((8,)),
            pltpu.SemaphoreType.DMA((N_SEMS,)),
            pltpu.SemaphoreType.DMA((N_SEMS,)),
            pltpu.SemaphoreType.REGULAR((3,)),
        ],
        compiler_params=pltpu.CompilerParams(
            collective_id=0, has_side_effects=True, vmem_limit_bytes=VMEM_LIMIT
        ),
        name="sigma_step",
    )(source, target, block_rows, block_cols, energy, wavefunction, left_ops, right_ops)
    return pl.pallas_call(
        finish_kernel,
        out_shape=(block, block),
        in_specs=[vmem] * 3,
        out_specs=(vmem, vmem),
        name="sigma_and_residual",
    )(*parts)


def solution(mesh):
    in_specs = (
        P(None, "rows", "cols"),
        P(),
        P(),
        P(),
        P("terms", "rows", None),
        P("terms", "cols", None),
        P("terms"),
        P("terms"),
    )
    out_specs = (P(None, "rows", "cols"), P(None, "rows", "cols"))
    return jax.shard_map(per_device, mesh=mesh, in_specs=in_specs, out_specs=out_specs, check_vma=False)
```
